32 devices in a mesh: tile: 8 (over z, y), date: 4 (over x, core).
Axes of the slice: x: 2, y: 2, z: 4, core: 2. Of those that a mesh axis runs over, the one named last changes fastest.
Arguments:
- complex_images: bfloat16 [8, 8, 8, 2, 10, 1920], P('date', 'tile')
- segment_position_map: int32 [8, 8], P('tile'), may hold values from 0 to 7, each once within a row
- usable_position_total: int32 [8], P('tile'), may hold values from 4 to 8
- interferogram_epochs: int32 [16, 2], replicated, may hold values from 0 to 7, as said below
Outputs:
- coherence: float32 [16, 2, 16, 1024], P('date', None, None, 'tile')
The draws below stay inside these ranges and needn't reach their ends.
Inputs may be any that keep to these rules, and one draw needn't show every extreme that they name: Each row of segment_position_map names every block position once. `interferogram_epochs`: the two dates of a pair differ.
All inputs are finite; a program needn't handle non-finite values.
Results may differ from the reference program's by a relative error of at most 0.0003.
Values may be sent and summed in bfloat16 or wider, within the bound.
A program may use at most 128 MiB of HBM per device.

```python
import math
import jax
import jax.numpy as jnp
from jax import lax

SEGMENT_HEIGHT = 10
RG_T = 1920
LOOK_RG = 15
LOOK_AZ = 5
EPOCH_TOTAL = 8
SEGMENT_TOTAL = 8
PATCH_TOTAL = 8
PAIRS = 16
LROWS = 16
LCOL = 128
NLCOL = 1024


def draw_complex_images(key, part):
    seeds = jax.random.split(key, 4)
    extent = (EPOCH_TOTAL, SEGMENT_TOTAL, PATCH_TOTAL, 2, SEGMENT_HEIGHT, RG_T)
    common = (1, SEGMENT_TOTAL, PATCH_TOTAL, 2, SEGMENT_HEIGHT, RG_T)
    shared_portion = jax.random.normal(seeds[0], common)
    noise = jax.random.normal(seeds[1], extent)
    weight = jnp.exp(jax.random.uniform(seeds[2], (EPOCH_TOTAL, 1, 1, 1, 1, 1), minval=math.log(0.3), maxval=math.log(2.0)))
    magnitude_entries = jnp.exp(jax.random.uniform(seeds[3], (1, SEGMENT_TOTAL, PATCH_TOTAL, 1, SEGMENT_HEIGHT, RG_T), minval=math.log(0.3), maxval=math.log(3.0)))
    return (magnitude_entries * (shared_portion + weight * noise)).astype(jnp.bfloat16)


def draw_interferogram_epochs(key, part):
    seeds = jax.random.split(key, 2)
    first = jax.random.randint(seeds[0], (PAIRS,), 0, EPOCH_TOTAL)
    offset = jax.random.randint(seeds[1], (PAIRS,), 1, EPOCH_TOTAL)
    second = (first + offset) % EPOCH_TOTAL
    return jnp.stack([first, second], axis=1).astype(jnp.int32)


def touch_ends(values, stream_key, smallest, top_value):
    dims = values.shape
    place = [jax.random.randint(jax.random.fold_in(stream_key, axis), (), 0, dims[axis]) for axis in range(len(dims))]
    values = values.at[tuple(place)].set(smallest)
    longest = dims.index(max(dims))
    place[longest] = (place[longest] + 1) % dims[longest]
    return values.at[tuple(place)].set(top_value)


def setup_inputs(seed: int = 0) -> dict:
    key_list = jax.random.split(jax.random.key(seed), 5)
    complex_images = draw_complex_images(jax.random.fold_in(key_list[4], 71), 0)
    segment_position_map = jax.vmap(lambda own: jax.random.permutation(own, SEGMENT_TOTAL))(jax.random.split(key_list[1], PATCH_TOTAL)).reshape((PATCH_TOTAL, SEGMENT_TOTAL)).astype(jnp.int32)
    usable_position_total = touch_ends(jax.random.randint(key_list[2], (PATCH_TOTAL,), SEGMENT_TOTAL // 2, SEGMENT_TOTAL + 1), jax.random.fold_in(key_list[2], 1), SEGMENT_TOTAL // 2, SEGMENT_TOTAL).astype(jnp.int32)
    interferogram_epochs = draw_interferogram_epochs(jax.random.fold_in(key_list[4], 71), 0)
    return {"complex_images": complex_images, "segment_position_map": segment_position_map, "usable_position_total": usable_position_total, "interferogram_epochs": interferogram_epochs}


EPS = 1e-05

def tile_looks(stack, first_idx, second_idx, valid, box):
    scale = 1.0 / (LOOK_AZ * LOOK_RG)

    def looks(values):
        ranged = jnp.dot(values, box, precision=lax.Precision.HIGHEST, preferred_element_type=jnp.float32)
        extent = ranged.shape
        return ranged.reshape(extent[:-2] + (extent[-2] // LOOK_AZ, LOOK_AZ, extent[-1])).sum(axis=-2) * scale

    def date_power(image):
        image = image.astype(jnp.float32)
        return looks(image[:, 0] * image[:, 0] + image[:, 1] * image[:, 1])
    power = lax.map(date_power, stack)

    def one_pair(indices):
        first = lax.dynamic_index_in_dim(stack, indices[0], 0, keepdims=False).astype(jnp.float32)
        second = lax.dynamic_index_in_dim(stack, indices[1], 0, keepdims=False).astype(jnp.float32)
        cross_re = looks(first[:, 0] * second[:, 0] + first[:, 1] * second[:, 1])
        cross_im = looks(first[:, 1] * second[:, 0] - first[:, 0] * second[:, 1])
        power_first = lax.dynamic_index_in_dim(power, indices[0], 0, keepdims=False)
        power_second = lax.dynamic_index_in_dim(power, indices[1], 0, keepdims=False)
        weight = valid[:, None, None] / jnp.sqrt((power_first + EPS) * (power_second + EPS))
        return jnp.stack([cross_re * weight, cross_im * weight], axis=0)
    return lax.map(one_pair, jnp.stack([first_idx, second_idx], axis=1).astype(jnp.int32))

def reference(complex_images, segment_position_map, usable_position_total, interferogram_epochs):
    box = (jnp.arange(RG_T)[:, None] // LOOK_RG == jnp.arange(LCOL)[None, :]).astype(jnp.float32)

    def one_tile(patch_ordinal):
        stack = lax.dynamic_index_in_dim(complex_images, patch_ordinal, 2, keepdims=False)
        positions = segment_position_map[patch_ordinal]
        valid = (positions < usable_position_total[patch_ordinal]).astype(jnp.float32)
        gamma = tile_looks(stack, interferogram_epochs[:, 0], interferogram_epochs[:, 1], valid, box)
        ranking = jnp.argsort(positions).astype(jnp.int32)
        gamma = jnp.take(gamma, ranking, axis=2)
        return gamma.reshape(PAIRS, 2, LROWS, LCOL)
    result = lax.map(one_tile, jnp.arange(PATCH_TOTAL, dtype=jnp.int32))
    return result.transpose(1, 2, 3, 0, 4).reshape(PAIRS, 2, LROWS, NLCOL)
```

```python
import functools

import jax
import jax.numpy as jnp
from jax import lax
from jax.experimental import pallas as pl
from jax.experimental.pallas import tpu as pltpu
from jax.sharding import PartitionSpec as P

LOOK_RG = 15
LOOK_AZ = 5
LANES = 128
EPS = 1e-05


def remote(src, dst, send_sem, recv_sem, tile, date):
    return pltpu.make_async_remote_copy(
        src_ref=src,
        dst_ref=dst,
        send_sem=send_sem,
        recv_sem=recv_sem,
        device_id={"tile": tile, "date": date},
        device_id_type=pl.DeviceIdType.MESH,
    )


def kernel(
    nt, nd, x_ref, pos_ref, usable_ref, ep_ref, out_ref,
    raw, plain, swapped, box, sums, looked, res, gath, rank_ref,
    send_sem, recv_sem, own_sem, res_send, res_recv, res_own,
):
    dates, tl, lines, padded, _, _ = raw.shape
    dl = dates // nd
    chunks = x_ref.shape[4]
    rows = 2 * padded
    pairs = ep_ref.shape[1]
    kl = pairs // nd
    looks = lines // LOOK_AZ
    i = lax.axis_index("tile")
    g = lax.axis_index("date")
    home = i // tl

    barrier = pltpu.get_barrier_semaphore()
    for s in range(1, nd):
        pl.semaphore_signal(
            barrier, inc=1, device_id={"tile": i, "date": lax.rem(g + s, nd)},
            device_id_type=pl.DeviceIdType.MESH,
        )

    def greet(b, carry):
        @pl.when(jnp.logical_or(b != i, home != g))
        def _():
            pl.semaphore_signal(
                barrier, inc=1, device_id={"tile": b, "date": home},
                device_id_type=pl.DeviceIdType.MESH,
            )
        return carry

    lax.fori_loop(0, nt, greet, 0)

    def own_copy(j):
        return pltpu.make_async_copy(
            x_ref.at[:, 0, g * tl + j], raw.at[pl.ds(g * dl, dl), j, :, pl.ds(0, chunks)],
            own_sem.at[j],
        )

    def raw_send(j, s):
        h = lax.rem(g + s, nd)
        return remote(
            x_ref.at[:, 0, h * tl + j], raw.at[pl.ds(g * dl, dl), j, :, pl.ds(0, chunks)],
            send_sem.at[j, s - 1], recv_sem.at[j, s - 1], i, h,
        )

    def raw_recv(j, s):
        h = lax.rem(g + nd - s, nd)
        return remote(
            x_ref.at[:, 0, j], raw.at[pl.ds(h * dl, dl), j, :, pl.ds(0, chunks)],
            send_sem.at[j, s - 1], recv_sem.at[j, s - 1], i, h,
        )

    for j in range(tl):
        own_copy(j).start()
    pl.semaphore_wait(barrier, nd - 1 + nd * tl - jnp.where(home == g, 1, 0))
    for j in range(tl):
        for s in range(1, nd):
            raw_send(j, s).start()

    col = lax.broadcasted_iota(jnp.int32, (LANES, LANES), 1) * LOOK_RG
    row = lax.broadcasted_iota(jnp.int32, (LANES, LANES), 0)
    for c in range(chunks):
        off = row + c * LANES - col
        box[c] = jnp.where(
            jnp.logical_and(off >= 0, off < LOOK_RG), 1.0, 0.0
        ).astype(jnp.bfloat16)

    def rank_of(p, carry):
        rank_ref[p] = lax.fori_loop(
            0, nt, lambda b, r: jnp.where(pos_ref[0, b] == p, b, r), 0
        )
        return carry

    lax.fori_loop(0, nt, rank_of, 0)

    view = raw.reshape(dates, tl, lines, rows, LANES)
    even = lax.broadcasted_iota(jnp.int32, (rows // 8, 8, LANES), 1) % 2 == 0
    items = 2 * pairs + dates

    def unpack(j, d):
        for a in range(looks):
            total = None
            for l in range(a * LOOK_AZ, (a + 1) * LOOK_AZ):
                v = view[d, j, l].astype(jnp.float32)
                plain[d, l] = v
                v8 = v.reshape(rows // 8, 8, LANES)
                swapped[d, l] = jnp.where(
                    even, -pltpu.roll(v8, 7, 1), pltpu.roll(v8, 1, 1)
                ).reshape(rows, LANES)
                total = v * v if total is None else total + v * v
            sums[pl.ds(((2 * pairs + d) * looks + a) * rows, rows)] = total

    def pair(k, carry):
        fa = ep_ref[0, k]
        fb = ep_ref[1, k]
        for a in range(looks):
            re = im = None
            for l in range(a * LOOK_AZ, (a + 1) * LOOK_AZ):
                va = plain[fa, l]
                tr = va * plain[fb, l]
                ti = va * swapped[fb, l]
                re = tr if re is None else re + tr
                im = ti if im is None else im + ti
            sums[pl.ds(pl.multiple_of(((2 * k) * looks + a) * rows, 8), rows)] = re
            sums[pl.ds(pl.multiple_of(((2 * k + 1) * looks + a) * rows, 8), rows)] = im
        return carry

    for j in range(tl):
        own_copy(j).wait()
        for s in range(1, nd):
            raw_recv(j, s).wait_recv()

        def unpack_step(d, carry):
            unpack(j, d)
            return carry

        lax.fori_loop(0, dates, unpack_step, 0)
        lax.fori_loop(0, pairs, pair, 0)
        n = items * looks
        acc = jnp.zeros((n, LANES), jnp.float32)
        for c in range(chunks):
            v = sums[pl.ds(2 * c, n, stride=rows)] + sums[pl.ds(2 * c + 1, n, stride=rows)]
            hi = v.astype(jnp.bfloat16)
            left = v - hi.astype(jnp.float32)
            mid = left.astype(jnp.bfloat16)
            low = (left - mid.astype(jnp.float32)).astype(jnp.bfloat16)
            for part in (hi, mid, low):
                acc = acc + jnp.dot(part, box[c], preferred_element_type=jnp.float32)
        acc = acc * (1.0 / (LOOK_AZ * LOOK_RG))
        for it in range(items):
            part = acc[it * looks:(it + 1) * looks]
            looked[it] = part if it < 2 * pairs else lax.rsqrt(part + EPS)
        for k in range(pairs):
            w = looked[2 * pairs + ep_ref[0, k]] * looked[2 * pairs + ep_ref[1, k]]
            res[j, k, 0] = looked[2 * k] * w
            res[j, k, 1] = looked[2 * k + 1] * w
        for h in range(nd):
            t = g * tl + j
            mine = jnp.logical_and(t == i, h == g)

            @pl.when(mine)
            def _():
                pltpu.make_async_copy(
                    res.at[j, pl.ds(h * kl, kl)], gath.at[i], res_own
                ).start()

            @pl.when(jnp.logical_not(mine))
            def _():
                remote(
                    res.at[j, pl.ds(h * kl, kl)], gath.at[i],
                    res_send.at[j, h], res_recv.at[i], t, h,
                ).start()

    def land(b, carry):
        here = jnp.logical_and(b == i, home == g)

        @pl.when(here)
        def _():
            pltpu.make_async_copy(res.at[0, pl.ds(0, kl)], gath.at[b], res_own).wait()

        @pl.when(jnp.logical_not(here))
        def _():
            remote(
                res.at[0, pl.ds(0, kl)], gath.at[b],
                res_send.at[0, 0], res_recv.at[b], i, g,
            ).wait_recv()
        return carry

    lax.fori_loop(0, nt, land, 0)
    for p in range(nt):
        valid = jnp.where(p < usable_ref[0], 1.0, 0.0).astype(jnp.float32)
        out_ref[:, :, p * looks:(p + 1) * looks, :] = gath[rank_ref[p]] * valid

    for j in range(tl):
        for s in range(1, nd):
            raw_send(j, s).wait_send()
        for h in range(nd):
            mine = jnp.logical_and(g * tl + j == i, h == g)

            @pl.when(jnp.logical_not(mine))
            def _():
                remote(
                    res.at[j, pl.ds(h * kl, kl)], gath.at[i],
                    res_send.at[j, h], res_recv.at[i], g * tl + j, h,
                ).wait_send()


def on_device(nt, nd, complex_images, segment_position_map, usable_position_total, interferogram_epochs):
    dl, bl, tiles, _, lines, width = complex_images.shape
    assert bl == 1 and tiles == nt
    chunks = width // LANES
    padded = -(-chunks // 8) * 8
    x = complex_images.reshape(dl, bl, tiles, 2, lines, chunks, LANES)
    x = x.transpose(0, 1, 2, 4, 5, 3, 6)
    dates = dl * nd
    tl = tiles // nd
    pairs = interferogram_epochs.shape[0]
    kl = pairs // nd
    looks = lines // LOOK_AZ
    items = 2 * pairs + dates
    dma = pltpu.SemaphoreType.DMA
    f32 = jnp.float32
    smem = pl.BlockSpec(memory_space=pltpu.SMEM)
    return pl.pallas_call(
        functools.partial(kernel, nt, nd),
        out_shape=jax.ShapeDtypeStruct((kl, 2, nt * looks, width // LOOK_RG), f32),
        in_specs=[pl.BlockSpec(memory_space=pltpu.HBM), smem, smem, smem],
        out_specs=pl.BlockSpec(memory_space=pltpu.VMEM),
        scratch_shapes=[
            pltpu.VMEM((dates, tl, lines, padded, 2, LANES), jnp.bfloat16),
            pltpu.VMEM((dates, lines, 2 * padded, LANES), f32),
            pltpu.VMEM((dates, lines, 2 * padded, LANES), f32),
            pltpu.VMEM((chunks, LANES, LANES), jnp.bfloat16),
            pltpu.VMEM((items * looks * 2 * padded, LANES), f32),
            pltpu.VMEM((items, looks, LANES), f32),
            pltpu.VMEM((tl, pairs, 2, looks, LANES), f32),
            pltpu.VMEM((nt, kl, 2, looks, LANES), f32),
            pltpu.SMEM((nt,), jnp.int32),
            dma((tl, nd - 1)),
            dma((tl, nd - 1)),
            dma((tl,)),
            dma((tl, nd)),
            dma((nt,)),
            dma,
        ],
        compiler_params=pltpu.CompilerParams(
            collective_id=0, has_side_effects=True, vmem_limit_bytes=48 * 1024 * 1024
        ),
        name="coherence",
    )(x, segment_position_map, usable_position_total, interferogram_epochs.T)


def solution(mesh):
    in_specs = (P("date", "tile", None, None, None, None), P("tile", None), P("tile"), P())
    out_specs = P("date", None, None, "tile")
    body = functools.partial(on_device, mesh.shape["tile"], mesh.shape["date"])
    return jax.shard_map(
        body, mesh=mesh, in_specs=in_specs, out_specs=out_specs, check_vma=False
    )
```

```python
import functools

import jax
import jax.numpy as jnp
from jax import lax
from jax.experimental import pallas as pl
from jax.experimental.pallas import tpu as pltpu
from jax.sharding import PartitionSpec as P

LOOK_RG = 15
LOOK_AZ = 5
LANES = 128
EPS = 1e-05


def remote(src, dst, send_sem, recv_sem, tile, date):
    return pltpu.make_async_remote_copy(
        src_ref=src,
        dst_ref=dst,
        send_sem=send_sem,
        recv_sem=recv_sem,
        device_id={"tile": tile, "date": date},
        device_id_type=pl.DeviceIdType.MESH,
    )


def bitwise_xor(a, b, bits):
    total = 0
    for s in range(bits):
        total = total + lax.rem(a // 2**s + b // 2**s, 2) * 2**s
    return total


def kernel(
    nt, nd, x_ref, pos_ref, usable_ref, ep_ref, out_ref,
    raw, plain, swapped, box, sums, looked, res, gath, rank_ref,
    send_sem, recv_sem, own_sem, res_send, res_recv, res_own, round_sem,
):
    dates, tl, lines, padded, _, _ = raw.shape
    dl = dates // nd
    chunks = x_ref.shape[4]
    rows = 2 * padded
    pairs = ep_ref.shape[1]
    kl = pairs // nd
    looks = lines // LOOK_AZ
    items = 2 * pairs + dates
    bits = nt.bit_length() - 1
    i = lax.axis_index("tile")
    g = lax.axis_index("date")

    def tile_of(j, h):
        return bitwise_xor(i, (tl - 1 - j) * nd + h, bits)

    def signal(sem, tile, date):
        pl.semaphore_signal(
            sem, inc=1, device_id={"tile": tile, "date": date},
            device_id_type=pl.DeviceIdType.MESH,
        )

    barrier = pltpu.get_barrier_semaphore()
    for r in range(bits):
        signal(barrier, bitwise_xor(i, 2**r, bits), g)
    for s in range(1, nd):
        signal(barrier, i, lax.rem(g + s, nd))

    def slot(date, j, a):
        return raw.at[
            pl.ds(date * dl, dl), j, pl.ds(a * LOOK_AZ, LOOK_AZ), pl.ds(0, chunks)
        ]

    def source(tile, a):
        return x_ref.at[:, 0, tile, pl.ds(a * LOOK_AZ, LOOK_AZ)]

    def own_copy(j, a):
        return pltpu.make_async_copy(source(tile_of(j, g), a), slot(g, j, a), own_sem.at[j, a])

    def raw_send(j, a, s):
        h = lax.rem(g + s, nd)
        return remote(
            source(tile_of(j, h), a), slot(g, j, a),
            send_sem.at[j, a, s - 1], recv_sem.at[j, a, s - 1], i, h,
        )

    def raw_recv(j, a, s):
        h = lax.rem(g + nd - s, nd)
        return remote(
            source(i, a), slot(h, j, a),
            send_sem.at[j, a, s - 1], recv_sem.at[j, a, s - 1], i, h,
        )

    parts = [(j, a) for j in range(tl) for a in range(looks)]
    for j, a in parts:
        own_copy(j, a).start()
    pl.semaphore_wait(barrier, nd - 1 + bits)
    for j, a in parts:
        for s in range(1, nd):
            raw_send(j, a, s).start()

    for r in range(bits):
        signal(round_sem.at[r], bitwise_xor(i, 2**r, bits), g)
        pl.semaphore_wait(round_sem.at[r], 1)

    col = lax.broadcasted_iota(jnp.int32, (LANES, LANES), 1) * LOOK_RG
    row = lax.broadcasted_iota(jnp.int32, (LANES, LANES), 0)
    for c in range(chunks):
        off = row + c * LANES - col
        box[pl.ds(c * LANES, LANES)] = jnp.where(
            jnp.logical_and(off >= 0, off < LOOK_RG), 1.0, 0.0
        ).astype(jnp.bfloat16)

    def rank_of(p, carry):
        rank_ref[p] = lax.fori_loop(
            0, nt, lambda b, r: jnp.where(pos_ref[0, b] == p, b, r), 0
        )
        return carry

    lax.fori_loop(0, nt, rank_of, 0)

    view = raw.reshape(dates, tl, lines, rows, LANES)
    even = lax.broadcasted_iota(jnp.int32, (rows // 8, 8, LANES), 1) % 2 == 0

    def unpack(j, a, d):
        total = None
        for l in range(LOOK_AZ):
            v = view[d, j, a * LOOK_AZ + l].astype(jnp.float32)
            plain[d, l] = v
            v8 = v.reshape(rows // 8, 8, LANES)
            swapped[d, l] = jnp.where(
                even, -pltpu.roll(v8, 7, 1), pltpu.roll(v8, 1, 1)
            ).reshape(rows, LANES)
            total = v * v if total is None else total + v * v
        sums[pl.ds(pl.multiple_of((2 * pairs + d) * rows, 8), rows)] = total

    def pair(k, carry):
        fa = ep_ref[0, k]
        fb = ep_ref[1, k]
        re = im = None
        for l in range(LOOK_AZ):
            va = plain[fa, l]
            tr = va * plain[fb, l]
            ti = va * swapped[fb, l]
            re = tr if re is None else re + tr
            im = ti if im is None else im + ti
        sums[pl.ds(pl.multiple_of(k * rows, 8), rows)] = re
        sums[pl.ds(pl.multiple_of((pairs + k) * rows, 8), rows)] = im
        return carry

    for j, a in parts:
        for s in range(nd):
            if s == 0:
                own_copy(j, a).wait()
            else:
                raw_recv(j, a, s).wait_recv()
            h = lax.rem(g + nd - s, nd)
            for d in range(dl):
                unpack(j, a, h * dl + d)
        lax.fori_loop(0, pairs, pair, 0)
        hi, low = [], []
        for c in range(chunks):
            v = (
                sums[pl.ds(2 * c, items, stride=rows)]
                + sums[pl.ds(2 * c + 1, items, stride=rows)]
            )
            top = v.astype(jnp.bfloat16)
            hi.append(top)
            low.append((v - top.astype(jnp.float32)).astype(jnp.bfloat16))
        weights = box[...]
        acc = jnp.dot(
            jnp.concatenate(hi, axis=1), weights, preferred_element_type=jnp.float32
        ) + jnp.dot(jnp.concatenate(low, axis=1), weights, preferred_element_type=jnp.float32)
        acc = acc * (1.0 / (LOOK_AZ * LOOK_RG))
        looked[pl.ds(0, 2 * pairs)] = acc[:2 * pairs]
        looked[pl.ds(2 * pairs, dates)] = lax.rsqrt(acc[2 * pairs:] + EPS)
        for k in range(pairs):
            w = (
                looked[pl.ds(2 * pairs + ep_ref[0, k], 1)]
                * looked[pl.ds(2 * pairs + ep_ref[1, k], 1)]
            )
            res[j, k, 0, a:a + 1] = looked[k:k + 1] * w
            res[j, k, 1, a:a + 1] = looked[pairs + k:pairs + k + 1] * w
        if a < looks - 1:
            continue
        t = tile_of(j, g)
        for h in range(nd):
            mine = jnp.logical_and(t == i, g == h)

            @pl.when(mine)
            def _():
                pltpu.make_async_copy(
                    res.at[j, pl.ds(h * kl, kl)], gath.at[i], res_own
                ).start()

            @pl.when(jnp.logical_not(mine))
            def _():
                remote(
                    res.at[j, pl.ds(h * kl, kl)], gath.at[i],
                    res_send.at[j, h], res_recv.at[i], t, h,
                ).start()

    def land(b, carry):
        here = jnp.logical_and(b == i, g == 0)

        @pl.when(here)
        def _():
            pltpu.make_async_copy(res.at[0, pl.ds(0, kl)], gath.at[b], res_own).wait()

        @pl.when(jnp.logical_not(here))
        def _():
            remote(
                res.at[0, pl.ds(0, kl)], gath.at[b],
                res_send.at[0, 0], res_recv.at[b], i, g,
            ).wait_recv()
        return carry

    lax.fori_loop(0, nt, land, 0)
    for p in range(nt):
        valid = jnp.where(p < usable_ref[0], 1.0, 0.0).astype(jnp.float32)
        out_ref[:, :, p * looks:(p + 1) * looks, :] = gath[rank_ref[p]] * valid

    for j, a in parts:
        for s in range(1, nd):
            raw_send(j, a, s).wait_send()
    for j in range(tl):
        for h in range(nd):
            t = tile_of(j, g)

            @pl.when(jnp.logical_not(jnp.logical_and(t == i, g == h)))
            def _():
                remote(
                    res.at[j, pl.ds(h * kl, kl)], gath.at[i],
                    res_send.at[j, h], res_recv.at[i], t, h,
                ).wait_send()


def on_device(nt, nd, complex_images, segment_position_map, usable_position_total, interferogram_epochs):
    dl, bl, tiles, _, lines, width = complex_images.shape
    assert bl == 1 and tiles == nt and nt & (nt - 1) == 0 and nt % nd == 0
    chunks = width // LANES
    padded = -(-chunks // 8) * 8
    x = complex_images.reshape(dl, bl, tiles, 2, lines, chunks, LANES)
    x = x.transpose(0, 1, 2, 4, 5, 3, 6)
    dates = dl * nd
    tl = tiles // nd
    pairs = interferogram_epochs.shape[0]
    kl = pairs // nd
    looks = lines // LOOK_AZ
    items = 2 * pairs + dates
    dma = pltpu.SemaphoreType.DMA
    f32 = jnp.float32
    smem = pl.BlockSpec(memory_space=pltpu.SMEM)
    return pl.pallas_call(
        functools.partial(kernel, nt, nd),
        out_shape=jax.ShapeDtypeStruct((kl, 2, nt * looks, width // LOOK_RG), f32),
        in_specs=[pl.BlockSpec(memory_space=pltpu.HBM), smem, smem, smem],
        out_specs=pl.BlockSpec(memory_space=pltpu.VMEM),
        scratch_shapes=[
            pltpu.VMEM((dates, tl, lines, padded, 2, LANES), jnp.bfloat16),
            pltpu.VMEM((dates, LOOK_AZ, 2 * padded, LANES), f32),
            pltpu.VMEM((dates, LOOK_AZ, 2 * padded, LANES), f32),
            pltpu.VMEM((chunks * LANES, width // LOOK_RG), jnp.bfloat16),
            pltpu.VMEM((items * 2 * padded, LANES), f32),
            pltpu.VMEM((items, LANES), f32),
            pltpu.VMEM((tl, pairs, 2, looks, LANES), f32),
            pltpu.VMEM((nt, kl, 2, looks, LANES), f32),
            pltpu.SMEM((nt,), jnp.int32),
            dma((tl, looks, nd - 1)),
            dma((tl, looks, nd - 1)),
            dma((tl, looks)),
            dma((tl, nd)),
            dma((nt,)),
            dma,
            pltpu.SemaphoreType.REGULAR((nt.bit_length() - 1,)),
        ],
        compiler_params=pltpu.CompilerParams(
            collective_id=0, has_side_effects=True
        ),
        name="coherence",
    )(x, segment_position_map, usable_position_total, interferogram_epochs.T)


def solution(mesh):
    in_specs = (P("date", "tile", None, None, None, None), P("tile", None), P("tile"), P())
    out_specs = P("date", None, None, "tile")
    body = functools.partial(on_device, mesh.shape["tile"], mesh.shape["date"])
    return jax.shard_map(
        body, mesh=mesh, in_specs=in_specs, out_specs=out_specs, check_vma=False
    )
```

```python
import functools

import jax
import jax.numpy as jnp
from jax import lax
from jax.experimental import pallas as pl
from jax.experimental.pallas import tpu as pltpu
from jax.sharding import PartitionSpec as P

LOOK_RG = 15
LOOK_AZ = 5
LANES = 128
EPS = 1e-05


def remote(src, dst, send_sem, recv_sem, tile, date):
    return pltpu.make_async_remote_copy(
        src_ref=src,
        dst_ref=dst,
        send_sem=send_sem,
        recv_sem=recv_sem,
        device_id={"tile": tile, "date": date},
        device_id_type=pl.DeviceIdType.MESH,
    )


def bitwise_xor(a, b, bits):
    total = 0
    for s in range(bits):
        total = total + lax.rem(a // 2**s + b // 2**s, 2) * 2**s
    return total


def kernel(
    nt, nd, x_ref, pos_hbm, usable_hbm, ep_hbm, out_ref,
    pos_ref, usable_ref, ep_ref, small_sem, raw, plain, swapped, box, sums, looked, res, gath, rank_ref,
    send_sem, recv_sem, own_sem, res_send, res_recv, res_own, round_sem,
):
    dates, tl, lines, padded, _, _ = raw.shape
    dl = dates // nd
    chunks = x_ref.shape[4]
    rows = 2 * padded
    pairs = ep_hbm.shape[1]
    kl = pairs // nd
    looks = lines // LOOK_AZ
    items = 2 * pairs + dates
    bits = nt.bit_length() - 1
    i = lax.axis_index("tile")
    g = lax.axis_index("date")

    def tile_of(j, h):
        return bitwise_xor(i, (tl - 1 - j) * nd + h, bits)

    def signal(sem, tile, date):
        pl.semaphore_signal(
            sem, inc=1, device_id={"tile": tile, "date": date},
            device_id_type=pl.DeviceIdType.MESH,
        )

    barrier = pltpu.get_barrier_semaphore()
    for s in range(1, nd):
        signal(barrier, i, lax.rem(g + s, nd))
    side = i + 1 - 2 * lax.rem(i, 2)
    signal(barrier, side, g)
    below = i >= 2
    above = i < nt - 2
    pl.when(below)(lambda: signal(barrier, i - 2, g))
    pl.when(above)(lambda: signal(barrier, i + 2, g))

    def slot(date, j, a):
        return raw.at[
            pl.ds(date * dl, dl), j, pl.ds(a * LOOK_AZ, LOOK_AZ), pl.ds(0, chunks)
        ]

    def source(tile, a):
        return x_ref.at[:, 0, tile, pl.ds(a * LOOK_AZ, LOOK_AZ)]

    def own_copy(j, a):
        return pltpu.make_async_copy(source(tile_of(j, g), a), slot(g, j, a), own_sem.at[j, a])

    def raw_send(j, a, s):
        h = lax.rem(g + s, nd)
        return remote(
            source(tile_of(j, h), a), slot(g, j, a),
            send_sem.at[j, a, s - 1], recv_sem.at[j, a, s - 1], i, h,
        )

    def raw_recv(j, a, s):
        h = lax.rem(g + nd - s, nd)
        return remote(
            source(i, a), slot(h, j, a),
            send_sem.at[j, a, s - 1], recv_sem.at[j, a, s - 1], i, h,
        )

    parts = [(j, a) for j in range(tl) for a in range(looks)]
    for j, a in parts:
        own_copy(j, a).start()
    pl.semaphore_wait(
        barrier, nd + jnp.where(below, 1, 0) + jnp.where(above, 1, 0)
    )
    for j, a in parts:
        for s in range(1, nd):
            raw_send(j, a, s).start()

    small = [
        pltpu.make_async_copy(src, dst, small_sem.at[n])
        for n, (src, dst) in enumerate(
            ((pos_hbm, pos_ref), (usable_hbm, usable_ref), (ep_hbm, ep_ref))
        )
    ]
    for copy in small:
        copy.start()

    signal(round_sem.at[0], side, g)
    pl.semaphore_wait(round_sem.at[0], 1)
    for step, ahead, behind in ((2, above, below), (-2, below, above)):
        sem = round_sem.at[1 if step > 0 else 2]
        pl.when(behind)(functools.partial(pl.semaphore_wait, sem, 1))
        pl.when(ahead)(functools.partial(signal, sem, i + step, g))

    for copy in small:
        copy.wait()

    col = lax.broadcasted_iota(jnp.int32, (LANES, LANES), 1) * LOOK_RG
    row = lax.broadcasted_iota(jnp.int32, (LANES, LANES), 0)
    for c in range(chunks):
        off = row + c * LANES - col
        box[pl.ds(c * LANES, LANES)] = jnp.where(
            jnp.logical_and(off >= 0, off < LOOK_RG), 1.0, 0.0
        ).astype(jnp.bfloat16)

    def rank_of(p, carry):
        rank_ref[p] = lax.fori_loop(
            0, nt, lambda b, r: jnp.where(pos_ref[0, b] == p, b, r), 0
        )
        return carry

    lax.fori_loop(0, nt, rank_of, 0)

    view = raw.reshape(dates, tl, lines, rows, LANES)
    even = lax.broadcasted_iota(jnp.int32, (rows // 8, 8, LANES), 1) % 2 == 0

    def unpack(j, a, d):
        total = None
        for l in range(LOOK_AZ):
            v = view[d, j, a * LOOK_AZ + l].astype(jnp.float32)
            plain[d, l] = v
            v8 = v.reshape(rows // 8, 8, LANES)
            swapped[d, l] = jnp.where(
                even, -pltpu.roll(v8, 7, 1), pltpu.roll(v8, 1, 1)
            ).reshape(rows, LANES)
            total = v * v if total is None else total + v * v
        sums[pl.ds(pl.multiple_of((2 * pairs + d) * rows, 8), rows)] = total

    def pair(k, carry):
        fa = ep_ref[0, k]
        fb = ep_ref[1, k]
        re = im = None
        for l in range(LOOK_AZ):
            va = plain[fa, l]
            tr = va * plain[fb, l]
            ti = va * swapped[fb, l]
            re = tr if re is None else re + tr
            im = ti if im is None else im + ti
        sums[pl.ds(pl.multiple_of(k * rows, 8), rows)] = re
        sums[pl.ds(pl.multiple_of((pairs + k) * rows, 8), rows)] = im
        return carry

    for j, a in parts:
        for s in range(nd):
            if s == 0:
                own_copy(j, a).wait()
            else:
                raw_recv(j, a, s).wait_recv()
            h = lax.rem(g + nd - s, nd)
            for d in range(dl):
                unpack(j, a, h * dl + d)
        lax.fori_loop(0, pairs, pair, 0)
        hi, low = [], []
        for c in range(chunks):
            v = (
                sums[pl.ds(2 * c, items, stride=rows)]
                + sums[pl.ds(2 * c + 1, items, stride=rows)]
            )
            top = v.astype(jnp.bfloat16)
            hi.append(top)
            low.append((v - top.astype(jnp.float32)).astype(jnp.bfloat16))
        weights = box[...]
        acc = jnp.dot(
            jnp.concatenate(hi, axis=1), weights, preferred_element_type=jnp.float32
        ) + jnp.dot(jnp.concatenate(low, axis=1), weights, preferred_element_type=jnp.float32)
        acc = acc * (1.0 / (LOOK_AZ * LOOK_RG))
        looked[pl.ds(0, 2 * pairs)] = acc[:2 * pairs]
        looked[pl.ds(2 * pairs, dates)] = lax.rsqrt(acc[2 * pairs:] + EPS)
        for k in range(pairs):
            w = (
                looked[pl.ds(2 * pairs + ep_ref[0, k], 1)]
                * looked[pl.ds(2 * pairs + ep_ref[1, k], 1)]
            )
            res[j, k, 0, a:a + 1] = looked[k:k + 1] * w
            res[j, k, 1, a:a + 1] = looked[pairs + k:pairs + k + 1] * w
        if a < looks - 1:
            continue
        t = tile_of(j, g)
        for h in range(nd):
            mine = jnp.logical_and(t == i, g == h)

            @pl.when(mine)
            def _():
                pltpu.make_async_copy(
                    res.at[j, pl.ds(h * kl, kl)], gath.at[i], res_own
                ).start()

            @pl.when(jnp.logical_not(mine))
            def _():
                remote(
                    res.at[j, pl.ds(h * kl, kl)], gath.at[i],
                    res_send.at[j, h], res_recv.at[i], t, h,
                ).start()

    def land(b, carry):
        here = jnp.logical_and(b == i, g == 0)

        @pl.when(here)
        def _():
            pltpu.make_async_copy(res.at[0, pl.ds(0, kl)], gath.at[b], res_own).wait()

        @pl.when(jnp.logical_not(here))
        def _():
            remote(
                res.at[0, pl.ds(0, kl)], gath.at[b],
                res_send.at[0, 0], res_recv.at[b], i, g,
            ).wait_recv()
        return carry

    lax.fori_loop(0, nt, land, 0)
    for p in range(nt):
        valid = jnp.where(p < usable_ref[0], 1.0, 0.0).astype(jnp.float32)
        out_ref[:, :, p * looks:(p + 1) * looks, :] = gath[rank_ref[p]] * valid

    for j, a in parts:
        for s in range(1, nd):
            raw_send(j, a, s).wait_send()
    for j in range(tl):
        for h in range(nd):
            t = tile_of(j, g)

            @pl.when(jnp.logical_not(jnp.logical_and(t == i, g == h)))
            def _():
                remote(
                    res.at[j, pl.ds(h * kl, kl)], gath.at[i],
                    res_send.at[j, h], res_recv.at[i], t, h,
                ).wait_send()


def on_device(nt, nd, complex_images, segment_position_map, usable_position_total, interferogram_epochs):
    dl, bl, tiles, _, lines, width = complex_images.shape
    assert bl == 1 and tiles == nt and nt & (nt - 1) == 0 and nt % nd == 0
    chunks = width // LANES
    padded = -(-chunks // 8) * 8
    x = complex_images.reshape(dl, bl, tiles, 2, lines, chunks, LANES)
    x = x.transpose(0, 1, 2, 4, 5, 3, 6)
    dates = dl * nd
    tl = tiles // nd
    pairs = interferogram_epochs.shape[0]
    kl = pairs // nd
    looks = lines // LOOK_AZ
    items = 2 * pairs + dates
    dma = pltpu.SemaphoreType.DMA
    f32 = jnp.float32
    return pl.pallas_call(
        functools.partial(kernel, nt, nd),
        out_shape=jax.ShapeDtypeStruct((kl, 2, nt * looks, width // LOOK_RG), f32),
        in_specs=[pl.BlockSpec(memory_space=pltpu.HBM)] * 4,
        out_specs=pl.BlockSpec(memory_space=pltpu.VMEM),
        scratch_shapes=[
            pltpu.SMEM((1, nt), jnp.int32),
            pltpu.SMEM((1,), jnp.int32),
            pltpu.SMEM((2, pairs), jnp.int32),
            dma((3,)),
            pltpu.VMEM((dates, tl, lines, padded, 2, LANES), jnp.bfloat16),
            pltpu.VMEM((dates, LOOK_AZ, 2 * padded, LANES), f32),
            pltpu.VMEM((dates, LOOK_AZ, 2 * padded, LANES), f32),
            pltpu.VMEM((chunks * LANES, width // LOOK_RG), jnp.bfloat16),
            pltpu.VMEM((items * 2 * padded, LANES), f32),
            pltpu.VMEM((items, LANES), f32),
            pltpu.VMEM((tl, pairs, 2, looks, LANES), f32),
            pltpu.VMEM((nt, kl, 2, looks, LANES), f32),
            pltpu.SMEM((nt,), jnp.int32),
            dma((tl, looks, nd - 1)),
            dma((tl, looks, nd - 1)),
            dma((tl, looks)),
            dma((tl, nd)),
            dma((nt,)),
            dma,
            pltpu.SemaphoreType.REGULAR((3,)),
        ],
        compiler_params=pltpu.CompilerParams(
            collective_id=0, has_side_effects=True
        ),
        name="coherence",
    )(x, segment_position_map, usable_position_total, interferogram_epochs.T)


def solution(mesh):
    in_specs = (P("date", "tile", None, None, None, None), P("tile", None), P("tile"), P())
    out_specs = P("date", None, None, "tile")
    body = functools.partial(on_device, mesh.shape["tile"], mesh.shape["date"])
    return jax.shard_map(
        body, mesh=mesh, in_specs=in_specs, out_specs=out_specs, check_vma=False
    )
```
